32 devices in a mesh: groups: 2 (over y), dp: 4 (over z), mp: 4 (over x, core).
Axes of the slice: x: 2, y: 2, z: 4, core: 2. Of those that a mesh axis runs over, the one named last changes fastest.
Arguments:
- tokens: bfloat16 [16384, 2048], P(('groups', 'dp'), 'mp'), parts along dimension 0, may hold values from -6 to 6
- x_weight: bfloat16 [2048, 2048], P(None, 'mp'), may hold values from -0.125 to 0.125
- z_weight: bfloat16 [2048, 2048], P(None, 'mp'), may hold values from -0.125 to 0.125
- bc_weight: bfloat16 [2048, 512], P(None, 'mp'), may hold values from -0.125 to 0.125
- dt_weight: bfloat16 [2048, 32], P(None, 'mp'), may hold values from -0.125 to 0.125
- dt_bias: float32 [32], P('mp'), may hold values from -3 to 1
- decay_rate: float32 [32], P('mp'), may hold values from 0.003 to 0.03
- norm_gain: float32 [2048], P('mp'), may hold values from 0.1 to 1.9
- out_weight: bfloat16 [2048, 2048], P('mp'), may hold values from -0.125 to 0.125
- store_states: bfloat16 [128, 131072], P(('groups', 'dp'), 'mp'), parts along dimension 0, may hold values from -6 to 6
- home_rows: int32 [128], P('groups'), parts along dimension 0, may hold values from 0 to 63, as said below
- event_counts: int32 [128], P(('groups', 'dp')), parts along dimension 0, may hold values from 1 to 128, as said below
Outputs:
- out_tokens: bfloat16 [16384, 2048], P(('groups', 'dp', 'mp')), parts along dimension 0
- new_store: bfloat16 [128, 131072], P(('groups', 'dp'), 'mp'), parts along dimension 0
The draws below stay inside these ranges and needn't reach their ends.
There are 2 independent parts, one for each index of `groups`. The reference program is written for one: setup_inputs(seed, part) draws one part's arguments, and reference() takes and returns one part's arrays. A program takes and returns all parts, laid end to end along the dimension named above; an argument that names none is the same for every part. Nothing has to cross between parts.
Inputs may be any that keep to these rules, and one draw needn't show every extreme that they name: A permutation: session r's state is row home_rows[r] of the store. The 16 sessions of one aligned block keep at most 4 states in one aligned block of 16 store rows, and every block of sessions reaches 4 in some block of rows. `event_counts`: event slots at or after a session's count are padding.
All inputs are finite; a program needn't handle non-finite values.
Results may differ from the reference program's by a relative error of at most 0.02.
Values may be sent and summed in bfloat16 or wider, within the bound.
A program may use at most 128 MiB of HBM per device.

```python
import math
import jax
import jax.numpy as jnp
from jax import lax

D = 2048
HEADS = 32
HEADDIM = 64
NSTATE = 64
GROUPS = 4
SPAN = 128
SES_DEV = 16
SESSIONS = 64
CAP = 4
INNER = 2048
N_DP = 4


def draw_home_rows(key, part):
    key_perm, key_fill, key_servers, key_store, key_place = jax.random.split(key, 5)
    lowest = max(1, (SES_DEV - N_DP + CAP - 2) // (CAP - 1))
    highest = SES_DEV // CAP
    full_pairs = jax.random.randint(key_fill, (), lowest, highest + 1)
    shard_order = jax.random.permutation(key_perm, N_DP)
    position = jnp.arange(SES_DEV, dtype=jnp.int32)
    paired = jnp.minimum(position // CAP, N_DP - 1)
    single = jnp.clip(full_pairs + position - full_pairs * CAP, 0, N_DP - 1)
    offset = shard_order[jnp.where(position < full_pairs * CAP, paired, single)]
    server_shift = jax.random.permutation(key_servers, N_DP)
    store_rotate = jax.random.randint(key_store, (N_DP,), 0, SES_DEV)
    place_rotate = jax.random.randint(key_place, (N_DP,), 0, SES_DEV)
    server = jnp.arange(N_DP, dtype=jnp.int32)[:, None]
    shard = (server_shift[server] + offset[None, :]) % N_DP
    slot = (position[None, :] + store_rotate[shard]) % SES_DEV
    place = (position[None, :] + place_rotate[server]) % SES_DEV
    target = (server * SES_DEV + place).reshape(-1)
    values = (shard * SES_DEV + slot).reshape(-1).astype(jnp.int32)
    return jnp.zeros((N_DP * SES_DEV,), jnp.int32).at[target].set(values)


def draw_event_counts(key, part):
    key_values, key_top, key_low = jax.random.split(key, 3)
    counts = jax.random.randint(key_values, (SESSIONS,), 1, SPAN + 1)
    top_index = jax.random.randint(key_top, (), 0, SESSIONS)
    low_index = (top_index + 1 + jax.random.randint(key_low, (), 0, SESSIONS - 1)) % SESSIONS
    counts = counts.at[top_index].set(SPAN)
    counts = counts.at[low_index].set(1)
    return counts.astype(jnp.int32)


def levels(own_key, dims, cuts, smallest, largest):
    def one(dim, parts):
        heights = jax.random.uniform(jax.random.fold_in(jax.random.fold_in(own_key, 6), dim), (parts,), jnp.float32, smallest / len(cuts), largest / len(cuts))
        return jnp.repeat(jnp.exp(heights), dims[dim] // parts).reshape((-1,) + (1,) * (len(dims) - dim - 1))

    factor_of = one(*cuts[0])
    for cut in cuts[1:]:
        factor_of = factor_of * one(*cut)
    return factor_of


def noise(rng, extent, width, bound, shards=(), kind=jnp.bfloat16):
    gain = levels(rng, extent, shards, -0.22, 0.18) if shards else 1.0
    result = jax.random.normal(rng, extent, jnp.float32) * width * gain
    return jnp.minimum(jnp.maximum(result, -bound), bound).astype(kind)


def setup_inputs(seed: int = 0, part: int = 0) -> dict:
    key_of = jax.random.split(jax.random.key(seed), 13)
    part_splits = jax.random.split(jax.random.fold_in(key_of[12], part), 13)
    tokens = noise(part_splits[0], (SESSIONS * SPAN, D), 1.0, 6.0, ((0, 4), (1, 4)))
    x_weight = noise(key_of[1], (D, INNER), D ** -0.5, 0.125, ((1, 4),))
    z_weight = noise(key_of[2], (D, INNER), D ** -0.5, 0.125, ((1, 4),))
    bc_weight = noise(key_of[3], (D, GROUPS * 2 * NSTATE), D ** -0.5, 0.125, ((1, 4),))
    dt_weight = noise(key_of[4], (D, HEADS), D ** -0.5, 0.125, ((1, 4),))
    dt_bias = jnp.clip(-3.0 + 4.0 * jax.random.uniform(key_of[5], (HEADS,), jnp.float32) ** levels(key_of[5], (HEADS,), ((0, 4),), -0.2, 0.2), -3.0, 1.0)
    decay_rate = jnp.clip(jnp.exp(math.log(0.03) - 2.3025851 * jax.random.uniform(key_of[6], (HEADS,), jnp.float32) ** levels(key_of[6], (HEADS,), ((0, 4),), -0.2, 0.2)), 0.003, 0.03)
    norm_gain = jnp.clip(1.0 + 0.18 * jax.random.normal(key_of[7], (INNER,), jnp.float32), 0.1, 1.9)
    out_weight = noise(key_of[8], (INNER, D), INNER ** -0.5, 0.125, ((0, 4),))
    store_states = noise(part_splits[9], (SESSIONS, HEADS * HEADDIM * NSTATE), 1.0, 6.0, ((0, 4), (1, 4)))
    home_rows = draw_home_rows(jax.random.fold_in(jax.random.fold_in(key_of[12], part), 71), part)
    event_counts = draw_event_counts(jax.random.fold_in(jax.random.fold_in(key_of[12], part), 71), part)
    return dict(tokens=tokens, x_weight=x_weight, z_weight=z_weight, bc_weight=bc_weight, dt_weight=dt_weight, dt_bias=dt_bias, decay_rate=decay_rate, norm_gain=norm_gain, out_weight=out_weight, store_states=store_states, home_rows=home_rows, event_counts=event_counts)


def rounded(values):
    return lax.optimization_barrier(values.astype(jnp.bfloat16)).astype(jnp.float32)

def group_scan(inputs, b_matrix, c_matrix, step_sizes, decay_rates, initial_state):
    decay_sum = jnp.cumsum(step_sizes * decay_rates[None, None, :], axis=1)
    causal_mask = jnp.arange(SPAN)[:, None] >= jnp.arange(SPAN)[None, :]
    lagged = jnp.transpose(decay_sum, (0, 2, 1))
    decay_gaps = jnp.where(causal_mask, lagged[:, :, :, None] - lagged[:, :, None, :], 0.0)
    kernel = jnp.einsum('stn,sun->stu', c_matrix, b_matrix)
    step_rows = jnp.transpose(step_sizes, (0, 2, 1))
    mixing = rounded(jnp.where(causal_mask, jnp.exp(-decay_gaps), 0.0) * step_rows[:, :, None, :] * kernel[:, None, :, :])
    diagonal_part = jnp.einsum('shtu,suhp->sthp', mixing, inputs)
    carried = jnp.einsum('stn,shpn->sthp', c_matrix, initial_state) * jnp.exp(-decay_sum)[:, :, :, None]
    final_decay = decay_sum[:, -1:, :]
    weighted = rounded(b_matrix[:, :, None, :] * (jnp.exp(-(final_decay - decay_sum)) * step_sizes)[:, :, :, None])
    new_state = jnp.exp(-final_decay[:, 0, :])[:, :, None, None] * initial_state + jnp.einsum('suhp,suhn->shpn', inputs, weighted)
    return (diagonal_part + carried, new_state)

def reference(tokens, x_weight, z_weight, bc_weight, dt_weight, dt_bias, decay_rate, norm_gain, out_weight, store_states, home_rows, event_counts):
    group_heads = HEADS // GROUPS
    group_width = group_heads * HEADDIM

    def one_block(block_index):
        first_row = (block_index * SES_DEV).astype(jnp.int32)
        token_rows = lax.dynamic_slice_in_dim(tokens, (first_row * SPAN).astype(jnp.int32), SES_DEV * SPAN, 0)
        wanted = lax.dynamic_slice_in_dim(home_rows, first_row, SES_DEV, 0)
        counts = lax.dynamic_slice_in_dim(event_counts, first_row, SES_DEV, 0)
        initial_all = jnp.take(store_states, wanted, axis=0).astype(jnp.float32).reshape(SES_DEV, HEADS, HEADDIM, NSTATE)
        inputs_all = rounded(jnp.dot(token_rows, x_weight, preferred_element_type=jnp.float32)).reshape(SES_DEV, SPAN, HEADS, HEADDIM)
        gate_values = rounded(jnp.dot(token_rows, z_weight, preferred_element_type=jnp.float32)).reshape(SES_DEV, SPAN, INNER)
        bc_values = rounded(jnp.dot(token_rows, bc_weight, preferred_element_type=jnp.float32)).reshape(SES_DEV, SPAN, GROUPS, 2, NSTATE)
        valid_mask = (jnp.arange(SPAN, dtype=jnp.int32)[None, :] < counts[:, None]).astype(jnp.float32)
        raw_steps = jnp.dot(token_rows, dt_weight, preferred_element_type=jnp.float32).reshape(SES_DEV, SPAN, HEADS)
        step_sizes = jax.nn.softplus(raw_steps + dt_bias[None, None, :]) * valid_mask[:, :, None]
        pieces_out = []
        pieces_state = []
        for group_index in range(GROUPS):
            head_range = slice(group_index * group_heads, (group_index + 1) * group_heads)
            outputs, new_state = group_scan(inputs_all[:, :, head_range], bc_values[:, :, group_index, 0], bc_values[:, :, group_index, 1], step_sizes[:, :, head_range], decay_rate[head_range], initial_all[:, head_range])
            channel_range = slice(group_index * group_width, (group_index + 1) * group_width)
            gated_values = outputs.reshape(SES_DEV, SPAN, group_width) * jax.nn.silu(gate_values[:, :, channel_range])
            inverse_rms = lax.rsqrt(lax.optimization_barrier(jnp.mean(gated_values * gated_values, axis=2, keepdims=True)) + 1e-05)
            pieces_out.append(gated_values * inverse_rms * norm_gain[channel_range][None, None, :] * valid_mask[:, :, None])
            pieces_state.append(new_state)
        normed = jnp.concatenate(pieces_out, axis=2).reshape(SES_DEV * SPAN, INNER).astype(jnp.bfloat16)
        out_block = jnp.dot(normed, out_weight, preferred_element_type=jnp.float32).astype(jnp.bfloat16)
        states_block = jnp.concatenate(pieces_state, axis=1).astype(jnp.bfloat16).reshape(SES_DEV, HEADS * HEADDIM * NSTATE)
        return (out_block, states_block)
    out_blocks, state_blocks = lax.map(one_block, jnp.arange(SESSIONS // SES_DEV, dtype=jnp.int32))
    out_tokens = out_blocks.reshape(SESSIONS * SPAN, D)
    new_store = jnp.zeros_like(store_states).at[home_rows].set(state_blocks.reshape(SESSIONS, HEADS * HEADDIM * NSTATE))
    return (out_tokens, new_store)
```

```python
import functools

import jax
import jax.numpy as jnp
from jax import lax
from jax.experimental import pallas as pl
from jax.experimental.pallas import tpu as pltpu
from jax.sharding import PartitionSpec as P

F32 = jnp.float32
BF16 = jnp.bfloat16


def rank_within(keys, order):
    earlier = (keys[None, :] == keys[:, None]) & (order[None, :] < order[:, None])
    return jnp.sum(earlier.astype(jnp.int32), axis=1)


def one_hot_rows(wanted, count):
    places = jnp.arange(count, dtype=jnp.int32)
    return (wanted[:, None] == places[None, :]).astype(BF16)


def chunk_kernel(
    heads,
    head_size,
    state_size,
    scalars,
    own_ref,
    sib_ref,
    far_ref,
    diag_ref,
    weight_ref,
    bias_ref,
    rate_ref,
    gain_ref,
    start_ref,
    normed_ref,
    state_ref,
    acc_ref,
):
    parts = own_ref.shape[0]
    slots = own_ref.shape[2]
    depth = own_ref.shape[3]
    inner = heads * head_size
    me = scalars[0]
    total = None
    for step, ref in enumerate((own_ref, sib_ref, far_ref, diag_ref)):
        rows = pl.ds(pl.multiple_of(jnp.bitwise_xor(me, step) * depth, depth), depth)
        piece = jnp.dot(
            ref[...].reshape(parts * slots, depth),
            weight_ref[rows, :],
            preferred_element_type=F32,
        )
        total = piece if total is None else total + piece
    acc_ref[...] = total

    lane = lax.broadcasted_iota(jnp.int32, (slots, slots), 1)
    row = lax.broadcasted_iota(jnp.int32, (slots, slots), 0)
    causal = row >= lane
    low = lane < head_size
    lane8 = lax.broadcasted_iota(jnp.int32, (heads, slots), 1)
    pair = 2 * head_size

    for step in range(parts):
        place = jnp.bitwise_xor(me, step)
        here = pl.ds(pl.multiple_of(place * slots, slots), slots)
        count = scalars[1 + step]
        slab = acc_ref[here, 2 * inner : 2 * inner + 128]
        b_f32 = slab[:, :state_size].astype(BF16).astype(F32)
        b_bf = slab[:, :state_size].astype(BF16)
        c_bf = acc_ref[here, 2 * inner + 128 : 2 * inner + 128 + state_size].astype(BF16)
        raw = slab.T[state_size : state_size + heads, :] + bias_ref[...]
        dt_t = jnp.maximum(raw, 0.0) + jnp.log1p(jnp.exp(-jnp.abs(raw)))
        dt_t = jnp.where(lane8 < count, dt_t, 0.0)
        cum_t = dt_t * rate_ref[...]
        shift = 1
        while shift < slots:
            moved = pltpu.roll(cum_t, shift, axis=1)
            cum_t = cum_t + jnp.where(lane8 >= shift, moved, 0.0)
            shift *= 2
        last = cum_t[:, slots - 1 : slots]
        weigh_t = jnp.exp(cum_t - last) * dt_t
        fade_t = jnp.exp(-cum_t)
        stacked = jnp.concatenate(
            [cum_t, weigh_t, fade_t, jnp.zeros((slots - 3 * heads, slots), F32)], axis=0
        ).T
        scores = lax.dot_general(
            c_bf, b_bf, (((1,), (1,)), ((), ())), preferred_element_type=F32
        )
        gated_parts = []
        squares = None
        for j in range(heads // 2):
            cols = slice(j * pair, (j + 1) * pair)
            xs = acc_ref[here, cols].astype(BF16)
            zs = acc_ref[here, inner + j * pair : inner + (j + 1) * pair].astype(BF16).astype(F32)
            split = jnp.concatenate(
                [jnp.where(low, xs, jnp.zeros((), BF16)), jnp.where(low, jnp.zeros((), BF16), xs)],
                axis=0,
            )
            mixes = []
            weighed = []
            for h in (2 * j, 2 * j + 1):
                gaps = jnp.where(causal, cum_t[h : h + 1, :] - stacked[:, h : h + 1], -1e30)
                mixes.append((jnp.exp(gaps) * dt_t[h : h + 1, :] * scores).astype(BF16))
                weighed.append((b_f32 * stacked[:, heads + h : heads + h + 1]).astype(BF16))
            y = jnp.dot(jnp.concatenate(mixes, axis=1), split, preferred_element_type=F32)
            start = start_ref[step, cols, :]
            carried = lax.dot_general(
                c_bf, start, (((1,), (1,)), ((), ())), preferred_element_type=F32
            )
            fade0 = stacked[:, 2 * heads + 2 * j : 2 * heads + 2 * j + 1]
            fade1 = stacked[:, 2 * heads + 2 * j + 1 : 2 * heads + 2 * j + 2]
            y = y + carried * jnp.where(low, fade0, fade1)
            grown = lax.dot_general(
                split,
                jnp.concatenate(weighed, axis=0),
                (((0,), (0,)), ((), ())),
                preferred_element_type=F32,
            )
            keep = jnp.where(
                row[:, :state_size] < head_size,
                fade_t[2 * j : 2 * j + 1, slots - 1 : slots],
                fade_t[2 * j + 1 : 2 * j + 2, slots - 1 : slots],
            )
            state_ref[step, cols, :] = (keep * start.astype(F32) + grown).astype(BF16)
            gated = y * (zs * jax.nn.sigmoid(zs))
            part = jnp.sum(gated * gated, axis=1, keepdims=True)
            squares = part if squares is None else squares + part
            gated_parts.append(gated)
        scale = lax.rsqrt(squares * (1.0 / inner) + 1e-05)
        scale = jnp.where(row[:, :1] < count, scale, 0.0)
        for j in range(heads // 2):
            cols = slice(j * pair, (j + 1) * pair)
            normed_ref[step, :, cols] = (gated_parts[j] * scale * gain_ref[:, cols]).astype(BF16)


def run_chunk(index, scalars, tokens4, sib, far, diag, weight, bias, rate, gain, start, heads, head_size, state_size):
    parts, _, slots, depth = tokens4.shape
    inner = heads * head_size
    width = weight.shape[1]
    chunk = pl.BlockSpec((parts, 1, slots, depth), lambda i, s: (0, 0, 0, 0))
    whole = lambda shape: pl.BlockSpec(shape, lambda i, s: (0,) * len(shape))
    rows = parts * slots
    return pl.pallas_call(
        functools.partial(chunk_kernel, heads, head_size, state_size),
        out_shape=(
            jax.ShapeDtypeStruct((parts, slots, inner), BF16),
            jax.ShapeDtypeStruct((parts, inner, state_size), BF16),
        ),
        grid_spec=pltpu.PrefetchScalarGridSpec(
            num_scalar_prefetch=1,
            grid=(1,),
            in_specs=[
                pl.BlockSpec((parts, 1, slots, depth), lambda i, s: (0, index, 0, 0)),
                chunk,
                chunk,
                chunk,
                whole(weight.shape),
                whole(bias.shape),
                whole(rate.shape),
                whole(gain.shape),
                pl.BlockSpec((parts, inner, state_size), lambda i, s: (index, 0, 0)),
            ],
            out_specs=(
                whole((parts, slots, inner)),
                whole((parts, inner, state_size)),
            ),
            scratch_shapes=[pltpu.VMEM((rows, width), F32)],
        ),
        compiler_params=pltpu.CompilerParams(vmem_limit_bytes=48 * 1024 * 1024),
        cost_estimate=pl.CostEstimate(
            flops=2 * rows * 4 * depth * width * 2,
            bytes_accessed=12 * 1024 * 1024,
            transcendentals=rows * heads * slots,
        ),
        name="chunk_layer",
    )(scalars, tokens4, sib, far, diag, weight, bias, rate, gain, start)


def body(
    tokens,
    x_weight,
    z_weight,
    bc_weight,
    dt_weight,
    dt_bias,
    decay_rate,
    norm_gain,
    out_weight,
    store_states,
    home_rows,
    event_counts,
):
    shard_count = lax.axis_size("dp")
    replica_count = lax.axis_size("groups")
    parts = lax.axis_size("mp")
    me = lax.axis_index("dp")
    part = lax.axis_index("mp").astype(jnp.int32)
    sessions = store_states.shape[0]
    state_width = store_states.shape[1]
    capacity = max(2, (sessions + shard_count - 1) // shard_count)
    slot_count = shard_count * capacity
    heads = dt_bias.shape[0]
    inner = x_weight.shape[1]
    head_size = inner // heads
    state_size = bc_weight.shape[1] // 2
    model = x_weight.shape[0]
    depth = tokens.shape[1]
    slots = tokens.shape[0] // sessions
    chunks = sessions // parts

    def swap(values, mask):
        return lax.ppermute(values, "mp", [(i, i ^ mask) for i in range(parts)])

    def shift_exchange(blocks):
        arrived = [blocks[0]]
        for k in range(1, shard_count):
            perm = [(i, (i + k) % shard_count) for i in range(shard_count)]
            arrived.append(lax.ppermute(blocks[k], "dp", perm))
        return jnp.concatenate(arrived, axis=0)

    tokens4 = tokens.reshape(parts, chunks, slots, depth)
    far_pieces = [swap(tokens4[:, j : j + 1], 2) for j in range(chunks)]

    positions = jnp.arange(sessions, dtype=jnp.int32)
    store_rows = me * sessions + positions
    everyone = jnp.arange(home_rows.shape[0], dtype=jnp.int32)
    owner = jnp.sum(
        (home_rows[None, :] == store_rows[:, None]).astype(jnp.int32) * everyone[None, :], axis=1
    )
    server = owner // sessions
    to_server = (server - me + shard_count) % shard_count
    row_slot = to_server * capacity + rank_within(server, positions)
    back_slot = row_slot
    wanted = lax.dynamic_slice_in_dim(home_rows, me * sessions, sessions)
    home_shard = wanted // sessions
    from_home = (me - home_shard + shard_count) % shard_count
    session_slot = from_home * capacity + rank_within(home_shard, wanted % sessions)

    pack = one_hot_rows(row_slot, slot_count).T
    outbound = jnp.dot(pack, store_states, preferred_element_type=F32).astype(BF16)
    inbound = shift_exchange(
        [outbound[k * capacity : (k + 1) * capacity] for k in range(shard_count)]
    )
    spots = jnp.arange(sessions, dtype=jnp.int32)
    chunk_order = jnp.bitwise_xor(spots % parts, part) * chunks + spots // parts
    unpack = one_hot_rows(session_slot[chunk_order], slot_count)
    start = (
        jnp.dot(unpack, inbound, preferred_element_type=F32)
        .astype(BF16)
        .reshape(sessions, inner, state_size)
    )

    pad_b = jnp.zeros((model, 128 - state_size - heads), BF16)
    pad_c = jnp.zeros((model, 128 - state_size), BF16)
    weight = jnp.concatenate(
        [
            x_weight,
            z_weight,
            bc_weight[:, :state_size],
            dt_weight,
            pad_b,
            bc_weight[:, state_size:],
            pad_c,
        ],
        axis=1,
    )
    ordered_counts = event_counts[chunk_order]

    replicas = replica_count * shard_count
    piece_rows = out_weight.shape[0] // replicas
    replica = lax.axis_index("groups") * shard_count + me
    piece = lax.dynamic_slice_in_dim(out_weight, replica * piece_rows, piece_rows, 0)
    piece = swap(piece, 2)
    far_out = lax.all_gather(piece, ("groups", "dp"), axis=0, tiled=True)
    sib_out = swap(out_weight, 1)
    diag_out = swap(far_out, 1)

    received = [[] for _ in range(parts)]
    states = []
    for j in range(chunks):
        far = far_pieces[j]
        sib = swap(tokens4[:, j : j + 1], 1)
        diag = swap(far, 1)
        scalars = jnp.concatenate([part[None], ordered_counts[j * parts : (j + 1) * parts]])
        normed, state = run_chunk(
            j,
            scalars,
            tokens4,
            sib,
            far,
            diag,
            weight,
            dt_bias[:, None],
            decay_rate[:, None],
            norm_gain[None, :],
            start,
            heads,
            head_size,
            state_size,
        )
        states.append(state)
        received[0].append(normed[0])
        for k in range(1, parts):
            received[k].append(swap(normed[k], k))
    new_state = jnp.concatenate(states, axis=0).reshape(sessions, state_width)
    slot_of = one_hot_rows(session_slot[chunk_order], slot_count).T
    outgoing = jnp.dot(slot_of, new_state, preferred_element_type=F32).astype(BF16)
    back = [outgoing[k * capacity : (k + 1) * capacity] for k in range(shard_count)]
    arrived = [back[0]]
    for k in range(1, shard_count):
        perm = [(i, (i - k) % shard_count) for i in range(shard_count)]
        arrived.append(lax.ppermute(back[k], "dp", perm))
    returned = jnp.concatenate(arrived, axis=0)
    new_store = jnp.dot(
        one_hot_rows(back_slot, slot_count), returned, preferred_element_type=F32
    ).astype(BF16)

    mixed = jnp.concatenate([jnp.concatenate(blocks, axis=0) for blocks in received], axis=1)
    out_full = jnp.concatenate([out_weight, sib_out, far_out, diag_out], axis=0)
    out_sum = jnp.dot(mixed, out_full, preferred_element_type=F32).astype(BF16)
    return (out_sum, new_store)


def solution(mesh):
    return jax.shard_map(
        body,
        mesh=mesh,
        in_specs=(
            P(("groups", "dp"), "mp"),
            P(None, "mp"),
            P(None, "mp"),
            P(None, "mp"),
            P(None, "mp"),
            P("mp"),
            P("mp"),
            P("mp"),
            P("mp", None),
            P(("groups", "dp"), "mp"),
            P("groups"),
            P(("groups", "dp")),
        ),
        out_specs=(P(("groups", "dp", "mp"), None), P(("groups", "dp"), "mp")),
        check_vma=False,
    )
```

```python
import functools

import jax
import jax.numpy as jnp
from jax import lax
from jax.experimental import pallas as pl
from jax.experimental.pallas import tpu as pltpu
from jax.sharding import PartitionSpec as P

F32 = jnp.float32
BF16 = jnp.bfloat16


def rank_within(keys, order):
    earlier = (keys[None, :] == keys[:, None]) & (order[None, :] < order[:, None])
    return jnp.sum(earlier.astype(jnp.int32), axis=1)


def one_hot_rows(wanted, count):
    places = jnp.arange(count, dtype=jnp.int32)
    return (wanted[:, None] == places[None, :]).astype(BF16)


def xor_place(me, mask):
    return lax.rem(lax.rem(me, 2) + mask % 2, 2) + 2 * lax.rem(me // 2 + mask // 2, 2)


def layer_kernel(
    heads,
    head_size,
    state_size,
    chunks,
    parts,
    shards,
    scalars,
    tokens_ref,
    outbound_ref,
    x_ref,
    z_ref,
    bd_ref,
    bias_ref,
    rate_ref,
    gain_ref,
    mixed_ref,
    state_ref,
    own,
    sib,
    far,
    diag,
    inbound,
    acc_ref,
    normed_ref,
    own_sem,
    sib_send,
    sib_recv,
    far_send,
    far_recv,
    diag_send,
    diag_recv,
    store_send,
    store_recv,
    store_local,
    norm_send,
    norm_recv,
    norm_local,
):
    slots = tokens_ref.shape[2]
    depth = tokens_ref.shape[3]
    inner = heads * head_size
    capacity = outbound_ref.shape[1]
    me = lax.axis_index("mp")
    dp = lax.axis_index("dp")
    MESH = pl.DeviceIdType.MESH

    barrier = pltpu.get_barrier_semaphore()
    for mask in range(1, parts):
        pl.semaphore_signal(
            barrier, inc=1, device_id={"mp": xor_place(me, mask)}, device_id_type=MESH
        )
    for k in range(1, shards):
        pl.semaphore_signal(
            barrier, inc=1, device_id={"dp": lax.rem(dp + k, shards)}, device_id_type=MESH
        )
    pl.semaphore_wait(barrier, parts - 1 + shards - 1)

    def remote(src, dst, send, recv, device):
        return pltpu.make_async_remote_copy(
            src_ref=src,
            dst_ref=dst,
            send_sem=send,
            recv_sem=recv,
            device_id=device,
            device_id_type=MESH,
        )

    def far_copy(j):
        return remote(
            tokens_ref.at[:, j], far.at[j], far_send.at[j], far_recv.at[j], {"mp": xor_place(me, 2)}
        )

    def sib_copy(j):
        return remote(
            tokens_ref.at[:, j], sib.at[j], sib_send.at[j], sib_recv.at[j], {"mp": xor_place(me, 1)}
        )

    def diag_copy(j):
        return remote(
            far.at[j], diag.at[j], diag_send.at[j], diag_recv.at[j], {"mp": xor_place(me, 1)}
        )

    def own_copy(j):
        return pltpu.make_async_copy(tokens_ref.at[:, j], own.at[j], own_sem.at[j])

    def store_copy(k):
        return remote(
            outbound_ref.at[k],
            inbound.at[k],
            store_send.at[k],
            store_recv.at[k],
            {"dp": lax.rem(dp + k, shards)},
        )

    store_here = pltpu.make_async_copy(outbound_ref.at[0], inbound.at[0], store_local)

    def norm_target(j, k):
        return mixed_ref.at[pl.ds(pl.multiple_of(j * slots, slots), slots), k * inner : (k + 1) * inner]

    def norm_copy(j, k):
        return remote(
            normed_ref.at[j, k],
            norm_target(j, k),
            norm_send.at[j, k],
            norm_recv.at[j, k],
            {"mp": xor_place(me, k)},
        )

    def norm_here(j):
        return pltpu.make_async_copy(normed_ref.at[j, 0], norm_target(j, 0), norm_local.at[j])

    ahead = min(2, chunks)
    for j in range(ahead):
        far_copy(j).start()
    for k in range(1, shards):
        store_copy(k).start()
    store_here.start()
    for j in range(chunks):
        own_copy(j).start()
        sib_copy(j).start()

    lane = lax.broadcasted_iota(jnp.int32, (slots, slots), 1)
    row = lax.broadcasted_iota(jnp.int32, (slots, slots), 0)
    causal = row >= lane
    low = lane < head_size
    lane8 = lax.broadcasted_iota(jnp.int32, (heads, slots), 1)
    pair = 2 * head_size

    def session(j, step):
        place = lax.rem(lax.rem(me, 2) + lax.rem(step, 2), 2) + 2 * lax.rem(me // 2 + step // 2, 2)
        here = pl.ds(pl.multiple_of(place * slots, slots), slots)
        index = j * parts + step
        count = scalars[index]
        spot = scalars[chunks * parts + index]
        spot_k = spot // capacity
        spot_c = spot - spot_k * capacity
        slab = acc_ref[here, 2 * inner : 2 * inner + 128]
        b_bf = slab[:, :state_size].astype(BF16)
        b_f32 = b_bf.astype(F32)
        c_bf = acc_ref[here, 2 * inner + 128 : 2 * inner + 128 + state_size].astype(BF16)
        raw = slab.T[state_size : state_size + heads, :] + bias_ref[...]
        dt_t = jnp.maximum(raw, 0.0) + jnp.log1p(jnp.exp(-jnp.abs(raw)))
        dt_t = jnp.where(lane8 < count, dt_t, 0.0)
        cum_t = dt_t * rate_ref[...]
        shift = 1
        while shift < slots:
            moved = pltpu.roll(cum_t, shift, axis=1)
            cum_t = cum_t + jnp.where(lane8 >= shift, moved, 0.0)
            shift *= 2
        last = cum_t[:, slots - 1 : slots]
        weigh_t = jnp.exp(cum_t - last) * dt_t
        fade_t = jnp.exp(-cum_t)
        stacked = jnp.concatenate(
            [cum_t, weigh_t, fade_t, jnp.zeros((slots - 3 * heads, slots), F32)], axis=0
        ).T
        scores = lax.dot_general(
            c_bf, b_bf, (((1,), (1,)), ((), ())), preferred_element_type=F32
        )
        gated_parts = []
        squares = None
        for g in range(heads // 2):
            cols = slice(g * pair, (g + 1) * pair)
            xs = acc_ref[here, cols].astype(BF16)
            zs = acc_ref[here, inner + g * pair : inner + (g + 1) * pair].astype(BF16).astype(F32)
            split = jnp.concatenate(
                [jnp.where(low, xs, jnp.zeros((), BF16)), jnp.where(low, jnp.zeros((), BF16), xs)],
                axis=0,
            )
            mixes = []
            weighed = []
            for h in (2 * g, 2 * g + 1):
                gaps = jnp.where(causal, cum_t[h : h + 1, :] - stacked[:, h : h + 1], -1e30)
                mixes.append((jnp.exp(gaps) * dt_t[h : h + 1, :] * scores).astype(BF16))
                weighed.append((b_f32 * stacked[:, heads + h : heads + h + 1]).astype(BF16))
            y = jnp.dot(jnp.concatenate(mixes, axis=1), split, preferred_element_type=F32)
            start = inbound[spot_k, spot_c, cols, :]
            carried = lax.dot_general(
                c_bf, start, (((1,), (1,)), ((), ())), preferred_element_type=F32
            )
            fade0 = stacked[:, 2 * heads + 2 * g : 2 * heads + 2 * g + 1]
            fade1 = stacked[:, 2 * heads + 2 * g + 1 : 2 * heads + 2 * g + 2]
            y = y + carried * jnp.where(low, fade0, fade1)
            grown = lax.dot_general(
                split,
                jnp.concatenate(weighed, axis=0),
                (((0,), (0,)), ((), ())),
                preferred_element_type=F32,
            )
            keep = jnp.where(
                row[:, :state_size] < head_size,
                fade_t[2 * g : 2 * g + 1, slots - 1 : slots],
                fade_t[2 * g + 1 : 2 * g + 2, slots - 1 : slots],
            )
            state_ref[index, cols, :] = (keep * start.astype(F32) + grown).astype(BF16)
            gated = y * (zs * jax.nn.sigmoid(zs))
            part = jnp.sum(gated * gated, axis=1, keepdims=True)
            squares = part if squares is None else squares + part
            gated_parts.append(gated)
        scale = lax.rsqrt(squares * (1.0 / inner) + 1e-05)
        scale = jnp.where(row[:, :1] < count, scale, 0.0)
        for g in range(heads // 2):
            cols = slice(g * pair, (g + 1) * pair)
            normed_ref[j, step, :, cols] = (gated_parts[g] * scale * gain_ref[:, cols]).astype(BF16)

    def compute(j):
        own_copy(j).wait()
        sib_copy(j).wait_recv()
        diag_copy(j).wait_recv()
        pieces = []
        for step, ref in enumerate((own, sib, far, diag)):
            rows = pl.ds(pl.multiple_of(xor_place(me, step) * depth, depth), depth)
            pieces.append((ref[j].reshape(parts * slots, depth), rows))
        base = 0
        for weight in (x_ref, z_ref, bd_ref):
            width = weight.shape[1]
            total = None
            for values, rows in pieces:
                piece = jnp.dot(values, weight[rows, :], preferred_element_type=F32)
                total = piece if total is None else total + piece
            acc_ref[:, base : base + width] = total
            base += width

        def run_session(step, carry):
            session(j, step)
            return carry

        lax.fori_loop(0, parts, run_session, 0)
        norm_here(j).start()
        for k in range(1, parts):
            norm_copy(j, k).start()

    def round_trip(j, carry):
        @pl.when(j < chunks)
        def _():
            far_copy(j).wait_recv()
            diag_copy(j).start()

        @pl.when(j + ahead < chunks)
        def _():
            far_copy(j + ahead).start()

        @pl.when(j == 1)
        def _():
            store_here.wait()
            for k in range(1, shards):
                store_copy(k).wait_recv()

        @pl.when(j > 0)
        def _():
            compute(j - 1)

        return carry

    lax.fori_loop(0, chunks + 1, round_trip, 0)

    for j in range(chunks):
        far_copy(j).wait_send()
        sib_copy(j).wait_send()
        diag_copy(j).wait_send()
        norm_here(j).wait()
        for k in range(1, parts):
            norm_copy(j, k).wait()
    for k in range(1, shards):
        store_copy(k).wait_send()


def run_layer(scalars, tokens4, outbound, x_weight, z_weight, bd_weight, bias, rate, gain, sizes, shards):
    heads, head_size, state_size = sizes
    parts, chunks, slots, depth = tokens4.shape
    inner = heads * head_size
    width = 2 * inner + bd_weight.shape[1]
    rows = parts * slots
    capacity = outbound.shape[1]
    vmem = pl.BlockSpec(memory_space=pltpu.VMEM)
    hbm = pl.BlockSpec(memory_space=pl.ANY)
    dma = pltpu.SemaphoreType.DMA
    block = pltpu.VMEM((chunks, parts, slots, depth), BF16)
    return pl.pallas_call(
        functools.partial(layer_kernel, heads, head_size, state_size, chunks, parts, shards),
        out_shape=(
            jax.ShapeDtypeStruct((chunks * slots, parts * inner), BF16),
            jax.ShapeDtypeStruct((chunks * parts, inner, state_size), BF16),
        ),
        in_specs=[pl.BlockSpec(memory_space=pltpu.SMEM), hbm, hbm] + [vmem] * 6,
        out_specs=(hbm, vmem),
        scratch_shapes=[
            block,
            block,
            block,
            block,
            pltpu.VMEM((shards, capacity, inner, state_size), BF16),
            pltpu.VMEM((rows, width), F32),
            pltpu.VMEM((chunks, parts, slots, inner), BF16),
            dma((chunks,)),
            dma((chunks,)),
            dma((chunks,)),
            dma((chunks,)),
            dma((chunks,)),
            dma((chunks,)),
            dma((chunks,)),
            dma((shards,)),
            dma((shards,)),
            dma,
            dma((chunks, parts)),
            dma((chunks, parts)),
            dma((chunks,)),
        ],
        compiler_params=pltpu.CompilerParams(
            vmem_limit_bytes=56 * 1024 * 1024, collective_id=0, has_side_effects=True
        ),
        cost_estimate=pl.CostEstimate(
            flops=2 * chunks * rows * 4 * depth * width * 4,
            bytes_accessed=64 * 1024 * 1024,
            transcendentals=chunks * rows * heads * slots,
        ),
        name="layer",
    )(scalars, tokens4, outbound, x_weight, z_weight, bd_weight, bias, rate, gain)


def project_kernel(mixed_ref, w0_ref, w1_ref, w2_ref, w3_ref, out_ref):
    depth = w0_ref.shape[0]
    total = None
    for k, ref in enumerate((w0_ref, w1_ref, w2_ref, w3_ref)):
        piece = jnp.dot(
            mixed_ref[:, k * depth : (k + 1) * depth], ref[...], preferred_element_type=F32
        )
        total = piece if total is None else total + piece
    out_ref[...] = total.astype(out_ref.dtype)


def project(mixed, weights):
    rows, depth = mixed.shape
    width = weights[0].shape[1]
    tile = min(512, width)
    return pl.pallas_call(
        project_kernel,
        out_shape=jax.ShapeDtypeStruct((rows, width), BF16),
        grid=(width // tile,),
        in_specs=[pl.BlockSpec((rows, depth), lambda i: (0, 0))]
        + [pl.BlockSpec((weights[0].shape[0], tile), lambda i: (0, i))] * 4,
        out_specs=pl.BlockSpec((rows, tile), lambda i: (0, i)),
        compiler_params=pltpu.CompilerParams(vmem_limit_bytes=40 * 1024 * 1024),
        cost_estimate=pl.CostEstimate(
            flops=2 * rows * depth * width, bytes_accessed=12 * 1024 * 1024, transcendentals=0
        ),
        name="project",
    )(mixed, *weights)


def body(
    tokens,
    x_weight,
    z_weight,
    bc_weight,
    dt_weight,
    dt_bias,
    decay_rate,
    norm_gain,
    out_weight,
    store_states,
    home_rows,
    event_counts,
):
    shard_count = lax.axis_size("dp")
    replica_count = lax.axis_size("groups")
    parts = lax.axis_size("mp")
    me = lax.axis_index("dp")
    part = lax.axis_index("mp").astype(jnp.int32)
    sessions = store_states.shape[0]
    state_width = store_states.shape[1]
    capacity = max(2, (sessions + shard_count - 1) // shard_count)
    slot_count = shard_count * capacity
    heads = dt_bias.shape[0]
    inner = x_weight.shape[1]
    head_size = inner // heads
    state_size = bc_weight.shape[1] // 2
    model = x_weight.shape[0]
    depth = tokens.shape[1]
    slots = tokens.shape[0] // sessions
    chunks = sessions // parts

    def swap(values, mask):
        return lax.ppermute(values, "mp", [(i, i ^ mask) for i in range(parts)])

    tokens4 = tokens.reshape(parts, chunks, slots, depth)

    positions = jnp.arange(sessions, dtype=jnp.int32)
    store_rows = me * sessions + positions
    everyone = jnp.arange(home_rows.shape[0], dtype=jnp.int32)
    owner = jnp.sum(
        (home_rows[None, :] == store_rows[:, None]).astype(jnp.int32) * everyone[None, :], axis=1
    )
    server = owner // sessions
    to_server = (server - me + shard_count) % shard_count
    row_slot = to_server * capacity + rank_within(server, positions)
    back_slot = row_slot
    wanted = lax.dynamic_slice_in_dim(home_rows, me * sessions, sessions)
    home_shard = wanted // sessions
    from_home = (me - home_shard + shard_count) % shard_count
    session_slot = from_home * capacity + rank_within(home_shard, wanted % sessions)

    pack = one_hot_rows(row_slot, slot_count).T
    outbound = jnp.dot(pack, store_states, preferred_element_type=F32).astype(BF16)
    outbound = outbound.reshape(shard_count, capacity, inner, state_size)
    spots = jnp.arange(sessions, dtype=jnp.int32)
    chunk_order = jnp.bitwise_xor(spots % parts, part) * chunks + spots // parts
    pad_b = jnp.zeros((model, 128 - state_size - heads), BF16)
    pad_c = jnp.zeros((model, 128 - state_size), BF16)
    bd_weight = jnp.concatenate(
        [bc_weight[:, :state_size], dt_weight, pad_b, bc_weight[:, state_size:], pad_c], axis=1
    )
    ordered_counts = event_counts[chunk_order]

    replicas = replica_count * shard_count
    piece_rows = out_weight.shape[0] // replicas
    replica = lax.axis_index("groups") * shard_count + me
    piece = lax.dynamic_slice_in_dim(out_weight, replica * piece_rows, piece_rows, 0)
    piece = swap(piece, 2)
    far_out = lax.all_gather(piece, ("groups", "dp"), axis=0, tiled=True)
    sib_out = swap(out_weight, 1)
    diag_out = swap(far_out, 1)

    scalars = jnp.concatenate([ordered_counts, session_slot[chunk_order]])
    mixed, new_state = run_layer(
        scalars,
        tokens4,
        outbound,
        x_weight,
        z_weight,
        bd_weight,
        dt_bias[:, None],
        decay_rate[:, None],
        norm_gain[None, :],
        (heads, head_size, state_size),
        shard_count,
    )
    new_state = new_state.reshape(sessions, state_width)
    slot_of = one_hot_rows(session_slot[chunk_order], slot_count).T
    outgoing = jnp.dot(slot_of, new_state, preferred_element_type=F32).astype(BF16)
    back = [outgoing[k * capacity : (k + 1) * capacity] for k in range(shard_count)]
    arrived = [back[0]]
    for k in range(1, shard_count):
        perm = [(i, (i - k) % shard_count) for i in range(shard_count)]
        arrived.append(lax.ppermute(back[k], "dp", perm))
    returned = jnp.concatenate(arrived, axis=0)
    new_store = jnp.dot(
        one_hot_rows(back_slot, slot_count), returned, preferred_element_type=F32
    ).astype(BF16)

    out_sum = project(mixed, (out_weight, sib_out, far_out, diag_out))
    return (out_sum, new_store)


def solution(mesh):
    return jax.shard_map(
        body,
        mesh=mesh,
        in_specs=(
            P(("groups", "dp"), "mp"),
            P(None, "mp"),
            P(None, "mp"),
            P(None, "mp"),
            P(None, "mp"),
            P("mp"),
            P("mp"),
            P("mp"),
            P("mp", None),
            P(("groups", "dp"), "mp"),
            P("groups"),
            P(("groups", "dp")),
        ),
        out_specs=(P(("groups", "dp", "mp"), None), P(("groups", "dp"), "mp")),
        check_vma=False,
    )
```

```python
import functools

import jax
import jax.numpy as jnp
from jax import lax
from jax.experimental import pallas as pl
from jax.experimental.pallas import tpu as pltpu
from jax.sharding import PartitionSpec as P

F32 = jnp.float32
BF16 = jnp.bfloat16


def rank_within(keys, order):
    earlier = (keys[None, :] == keys[:, None]) & (order[None, :] < order[:, None])
    return jnp.sum(earlier.astype(jnp.int32), axis=1)


def xor_place(me, mask):
    return lax.rem(lax.rem(me, 2) + mask % 2, 2) + 2 * lax.rem(me // 2 + mask // 2, 2)


def layer_kernel(
    heads,
    head_size,
    state_size,
    chunks,
    parts,
    shards,
    scalars,
    tokens_ref,
    store_ref,
    x_ref,
    z_ref,
    bc_ref,
    dtw_ref,
    bias_ref,
    rate_ref,
    gain_ref,
    outw_ref,
    out_ref,
    new_store_ref,
    own,
    sib,
    far,
    diag,
    outbound,
    inbound,
    state_ref,
    outgoing,
    returned,
    acc_ref,
    normed_ref,
    own_sum,
    far_part,
    pair_out,
    pair_in,
    far_out,
    far_in,
    own_sem,
    sib_send,
    sib_recv,
    far_send,
    far_recv,
    diag_send,
    diag_recv,
    store_send,
    store_recv,
    back_send,
    back_recv,
    pair_send,
    pair_recv,
    sum_send,
    sum_recv,
):
    slots = tokens_ref.shape[2]
    depth = tokens_ref.shape[3]
    inner = heads * head_size
    sessions = chunks * parts
    capacity = outbound.shape[1]
    me = lax.axis_index("mp")
    dp = lax.axis_index("dp")
    MESH = pl.DeviceIdType.MESH

    barrier = pltpu.get_barrier_semaphore()
    for mask in range(1, parts):
        pl.semaphore_signal(
            barrier, inc=1, device_id={"mp": xor_place(me, mask)}, device_id_type=MESH
        )
    for k in range(1, shards):
        pl.semaphore_signal(
            barrier, inc=1, device_id={"dp": lax.rem(dp + k, shards)}, device_id_type=MESH
        )
    pl.semaphore_wait(barrier, parts - 1 + shards - 1)

    def remote(src, dst, send, recv, device):
        return pltpu.make_async_remote_copy(
            src_ref=src,
            dst_ref=dst,
            send_sem=send,
            recv_sem=recv,
            device_id=device,
            device_id_type=MESH,
        )

    def far_copy(j):
        return remote(
            tokens_ref.at[:, j], far.at[j], far_send.at[j], far_recv.at[j], {"mp": xor_place(me, 2)}
        )

    def sib_copy(j):
        return remote(
            tokens_ref.at[:, j], sib.at[j], sib_send.at[j], sib_recv.at[j], {"mp": xor_place(me, 1)}
        )

    def diag_copy(j):
        return remote(
            far.at[j], diag.at[j], diag_send.at[j], diag_recv.at[j], {"mp": xor_place(me, 1)}
        )

    def own_copy(j):
        return pltpu.make_async_copy(tokens_ref.at[:, j], own.at[j], own_sem.at[j])

    def store_copy(k):
        return remote(
            outbound.at[k],
            inbound.at[k],
            store_send.at[k],
            store_recv.at[k],
            {"dp": lax.rem(dp + k, shards)},
        )

    def back_copy(k):
        return remote(
            outgoing.at[k],
            returned.at[k],
            back_send.at[k],
            back_recv.at[k],
            {"dp": lax.rem(dp + shards - k, shards)},
        )

    def pair_copy(j):
        return remote(
            pair_out.at[j], pair_in.at[j], pair_send.at[j], pair_recv.at[j], {"mp": xor_place(me, 1)}
        )

    def sum_copy(j):
        return remote(
            far_out.at[j], far_in.at[j], sum_send.at[j], sum_recv.at[j], {"mp": xor_place(me, 2)}
        )

    ahead = min(2, chunks)
    for j in range(ahead):
        far_copy(j).start()
    for j in range(chunks):
        own_copy(j).start()
        sib_copy(j).start()

    def fill_outbound(k):
        for c in range(capacity):
            outbound[k, c] = store_ref[scalars[2 * sessions + k * capacity + c]]

    for k in range(1, shards):
        fill_outbound(k)
        store_copy(k).start()
    for c in range(capacity):
        inbound[0, c] = store_ref[scalars[2 * sessions + c]]

    eye = lax.broadcasted_iota(jnp.int32, (heads, heads), 0) == lax.broadcasted_iota(
        jnp.int32, (heads, heads), 1
    )
    rate_col = jnp.sum(jnp.where(eye, rate_ref[...], 0.0), axis=1, keepdims=True)
    bias_col = jnp.sum(jnp.where(eye, bias_ref[...], 0.0), axis=1, keepdims=True)
    lane = lax.broadcasted_iota(jnp.int32, (slots, slots), 1)
    row = lax.broadcasted_iota(jnp.int32, (slots, slots), 0)
    causal = row >= lane
    low = lane < head_size
    lane8 = lax.broadcasted_iota(jnp.int32, (heads, slots), 1)
    pair = 2 * head_size
    tile = min(512, out_ref.shape[1])
    spread = (row == 2 * (lane % head_size) + lane // head_size).astype(BF16)

    def session(j, step):
        place = lax.rem(lax.rem(me, 2) + lax.rem(step, 2), 2) + 2 * lax.rem(me // 2 + step // 2, 2)
        here = pl.ds(pl.multiple_of(place * slots, slots), slots)
        index = place * chunks + j
        count = scalars[index]
        spot = scalars[sessions + index]
        spot_k = spot // capacity
        spot_c = spot - spot_k * capacity
        bc = acc_ref[here, 2 * inner : 2 * inner + 2 * state_size]
        b_bf = bc[:, :state_size].astype(BF16)
        b_f32 = b_bf.astype(F32)
        c_bf = bc[:, state_size:].astype(BF16)
        slab = acc_ref[here, 2 * inner + 2 * state_size : 2 * inner + 2 * state_size + 128]
        raw = slab.T[:heads, :] + bias_col
        dt_t = jnp.maximum(raw, 0.0) + jnp.log1p(jnp.exp(-jnp.abs(raw)))
        dt_t = jnp.where(lane8 < count, dt_t, 0.0)
        cum_t = dt_t * rate_col
        shift = 1
        while shift < slots:
            moved = pltpu.roll(cum_t, shift, axis=1)
            cum_t = cum_t + jnp.where(lane8 >= shift, moved, 0.0)
            shift *= 2
        last = cum_t[:, slots - 1 : slots]
        weigh_t = jnp.exp(cum_t - last) * dt_t
        fade_t = jnp.exp(-cum_t)
        stacked = jnp.concatenate(
            [cum_t, weigh_t, fade_t, jnp.zeros((slots - 3 * heads, slots), F32)], axis=0
        ).T
        scores = lax.dot_general(
            c_bf, b_bf, (((1,), (1,)), ((), ())), preferred_element_type=F32
        )
        gated_parts = []
        squares = None
        for g in range(heads // 2):
            cols = slice(g * pair, (g + 1) * pair)
            xs = acc_ref[here, cols].astype(BF16)
            zs = acc_ref[here, inner + g * pair : inner + (g + 1) * pair].astype(BF16).astype(F32)
            split = jnp.concatenate(
                [jnp.where(low, xs, jnp.zeros((), BF16)), jnp.where(low, jnp.zeros((), BF16), xs)],
                axis=0,
            )
            mixes = []
            weighed = []
            for h in (2 * g, 2 * g + 1):
                gaps = jnp.where(causal, cum_t[h : h + 1, :] - stacked[:, h : h + 1], -1e30)
                mixes.append((jnp.exp(gaps) * dt_t[h : h + 1, :] * scores).astype(BF16))
                weighed.append((b_f32 * stacked[:, heads + h : heads + h + 1]).astype(BF16))
            y = jnp.dot(jnp.concatenate(mixes, axis=1), split, preferred_element_type=F32)
            rows = slice(g * head_size, (g + 1) * head_size)
            kept = inbound[spot_k, spot_c, rows, :]
            halves = jnp.concatenate([kept[:, :state_size], kept[:, state_size:]], axis=0)
            start = jnp.dot(spread, halves, preferred_element_type=F32).astype(BF16)
            carried = lax.dot_general(
                c_bf, start, (((1,), (1,)), ((), ())), preferred_element_type=F32
            )
            fade0 = stacked[:, 2 * heads + 2 * g : 2 * heads + 2 * g + 1]
            fade1 = stacked[:, 2 * heads + 2 * g + 1 : 2 * heads + 2 * g + 2]
            y = y + carried * jnp.where(low, fade0, fade1)
            grown = lax.dot_general(
                jnp.dot(split, spread, preferred_element_type=F32).astype(BF16),
                jnp.concatenate(weighed, axis=0),
                (((0,), (0,)), ((), ())),
                preferred_element_type=F32,
            )
            keep = jnp.where(
                row[:head_size] < head_size // 2,
                fade_t[2 * g : 2 * g + 1, slots - 1 : slots],
                fade_t[2 * g + 1 : 2 * g + 2, slots - 1 : slots],
            )
            grown = jnp.concatenate([grown[:head_size], grown[head_size:]], axis=1)
            state_ref[index, rows, :] = (keep * kept.astype(F32) + grown).astype(BF16)
            gated = y * (zs * jax.nn.sigmoid(zs))
            part = jnp.sum(gated * gated, axis=1, keepdims=True)
            squares = part if squares is None else squares + part
            gated_parts.append(gated)
        scale = lax.rsqrt(squares * (1.0 / inner) + 1e-05)
        scale = jnp.where(row[:, :1] < count, scale, 0.0)
        for g in range(heads // 2):
            cols = slice(g * pair, (g + 1) * pair)
            normed_ref[pl.ds(pl.multiple_of(step * slots, slots), slots), cols] = (gated_parts[g] * scale * gain_ref[:, cols]).astype(BF16)

    def compute(j):
        own_copy(j).wait()
        sib_copy(j).wait_recv()
        diag_copy(j).wait_recv()
        pieces = []
        for step, ref in enumerate((own, sib, far, diag)):
            rows = pl.ds(pl.multiple_of(xor_place(me, step) * depth, depth), depth)
            pieces.append((ref[j].reshape(parts * slots, depth), rows))
        base = 0
        for weight in (x_ref, z_ref, bc_ref, dtw_ref):
            width = weight.shape[1]
            total = None
            for values, rows in pieces:
                piece = jnp.dot(values, weight[rows, :], preferred_element_type=F32)
                total = piece if total is None else total + piece
            if width < 128:
                total = jnp.concatenate(
                    [total, jnp.zeros((total.shape[0], 128 - width), F32)], axis=1
                )
                width = 128
            acc_ref[:, base : base + width] = total
            base += width

        @pl.when(j > 0)
        def _():
            combine(j - 1)

        def run_session(step, carry):
            session(j, step)
            return carry

        lax.fori_loop(0, parts, run_session, 0)

        @pl.loop(0, out_ref.shape[1] // tile)
        def _(t):
            cols = pl.ds(pl.multiple_of(t * tile, tile), tile)
            part = jnp.dot(normed_ref[...], outw_ref[:, cols], preferred_element_type=F32)
            own_sum[j, :, cols] = part[:slots]
            pair_out[j, 0, :, cols] = part[slots : 2 * slots].astype(BF16)
            far_part[:, cols] = part[2 * slots : 3 * slots]
            pair_out[j, 1, :, cols] = part[3 * slots :].astype(BF16)

        pair_copy(j).start()

    def combine(j):
        pair_copy(j).wait_recv()
        far_out[j] = (far_part[...] + pair_in[j, 1].astype(F32)).astype(BF16)
        sum_copy(j).start()

    def round_trip(j, carry):
        @pl.when(j < chunks)
        def _():
            far_copy(j).wait_recv()
            diag_copy(j).start()

        @pl.when(j + ahead < chunks)
        def _():
            far_copy(j + ahead).start()

        @pl.when(j == 1)
        def _():
            for k in range(1, shards):
                store_copy(k).wait_recv()

        @pl.when(j > 0)
        def _():
            compute(j - 1)

        return carry

    lax.fori_loop(0, chunks + 1, round_trip, 0)

    for k in range(1, shards):
        for c in range(capacity):
            outgoing[k, c] = state_ref[scalars[2 * sessions + shards * capacity + k * capacity + c]]
        back_copy(k).start()
    for c in range(capacity):
        returned[0, c] = state_ref[scalars[2 * sessions + shards * capacity + c]]
    combine(chunks - 1)

    for j in range(chunks):
        sum_copy(j).wait_recv()
        rows = slice(j * slots, (j + 1) * slots)
        out_ref[rows, :] = (
            own_sum[j] + pair_in[j, 0].astype(F32) + far_in[j].astype(F32)
        ).astype(BF16)

    for k in range(1, shards):
        back_copy(k).wait_recv()
    for r in range(sessions):
        spot = scalars[2 * sessions + 2 * shards * capacity + r]
        spot_k = spot // capacity
        new_store_ref[r] = returned[spot_k, spot - spot_k * capacity]

    for j in range(chunks):
        far_copy(j).wait_send()
        sib_copy(j).wait_send()
        diag_copy(j).wait_send()
        pair_copy(j).wait_send()
        sum_copy(j).wait_send()
    for k in range(1, shards):
        store_copy(k).wait_send()
        back_copy(k).wait_send()


def run_layer(scalars, tokens4, store, weights, params, out_weight, sizes, shards, capacity):
    heads, head_size, state_size = sizes
    parts, chunks, slots, depth = tokens4.shape
    inner = heads * head_size
    width = 2 * inner + 2 * state_size + 128
    rows = parts * slots
    model = out_weight.shape[1]
    packed = store.shape[1:]
    vmem = pl.BlockSpec(memory_space=pltpu.VMEM)
    hbm = pl.BlockSpec(memory_space=pl.ANY)
    dma = pltpu.SemaphoreType.DMA
    block = pltpu.VMEM((chunks, parts, slots, depth), BF16)
    exchange = pltpu.VMEM((shards, capacity) + packed, BF16)
    return pl.pallas_call(
        functools.partial(layer_kernel, heads, head_size, state_size, chunks, parts, shards),
        out_shape=(
            jax.ShapeDtypeStruct((chunks * slots, model), BF16),
            jax.ShapeDtypeStruct(store.shape, BF16),
        ),
        in_specs=[pl.BlockSpec(memory_space=pltpu.SMEM), hbm] + [vmem] * 9,
        out_specs=(vmem, vmem),
        scratch_shapes=[
            block,
            block,
            block,
            block,
            exchange,
            exchange,
            pltpu.VMEM((chunks * parts,) + packed, BF16),
            exchange,
            exchange,
            pltpu.VMEM((rows, width), F32),
            pltpu.VMEM((rows, inner), BF16),
            pltpu.VMEM((chunks, slots, model), F32),
            pltpu.VMEM((slots, model), F32),
            pltpu.VMEM((chunks, 2, slots, model), BF16),
            pltpu.VMEM((chunks, 2, slots, model), BF16),
            pltpu.VMEM((chunks, slots, model), BF16),
            pltpu.VMEM((chunks, slots, model), BF16),
        ]
        + [dma((chunks,))] * 7
        + [dma((shards,))] * 4
        + [dma((chunks,))] * 4,
        compiler_params=pltpu.CompilerParams(
            vmem_limit_bytes=62 * 1024 * 1024, collective_id=0, has_side_effects=True
        ),
        cost_estimate=pl.CostEstimate(
            flops=2 * chunks * rows * 4 * depth * width * 4,
            bytes_accessed=64 * 1024 * 1024,
            transcendentals=chunks * rows * heads * slots,
        ),
        name="layer",
    )(scalars, tokens4, store, *weights, *params, out_weight)


def body(
    tokens,
    x_weight,
    z_weight,
    bc_weight,
    dt_weight,
    dt_bias,
    decay_rate,
    norm_gain,
    out_weight,
    store_states,
    home_rows,
    event_counts,
):
    shard_count = lax.axis_size("dp")
    parts = lax.axis_size("mp")
    me = lax.axis_index("dp")
    sessions = store_states.shape[0]
    state_width = store_states.shape[1]
    capacity = max(2, (sessions + shard_count - 1) // shard_count)
    slot_count = shard_count * capacity
    heads = dt_bias.shape[0]
    inner = x_weight.shape[1]
    head_size = inner // heads
    state_size = bc_weight.shape[1] // 2
    depth = tokens.shape[1]
    slots = tokens.shape[0] // sessions
    chunks = sessions // parts

    tokens4 = tokens.reshape(parts, chunks, slots, depth)

    positions = jnp.arange(sessions, dtype=jnp.int32)
    store_rows = me * sessions + positions
    everyone = jnp.arange(home_rows.shape[0], dtype=jnp.int32)
    owner = jnp.sum(
        (home_rows[None, :] == store_rows[:, None]).astype(jnp.int32) * everyone[None, :], axis=1
    )
    server = owner // sessions
    to_server = (server - me + shard_count) % shard_count
    row_slot = to_server * capacity + rank_within(server, positions)
    wanted = lax.dynamic_slice_in_dim(home_rows, me * sessions, sessions)
    home_shard = wanted // sessions
    from_home = (me - home_shard + shard_count) % shard_count
    session_slot = from_home * capacity + rank_within(home_shard, wanted % sessions)

    all_slots = jnp.arange(slot_count, dtype=jnp.int32)

    def holder(slot_of):
        chosen = slot_of[None, :] == all_slots[:, None]
        return jnp.sum(chosen.astype(jnp.int32) * positions[None, :], axis=1)

    scalars = jnp.concatenate(
        [event_counts, session_slot, holder(row_slot), holder(session_slot), row_slot]
    )
    out_sum, new_store = run_layer(
        scalars,
        tokens4,
        store_states.reshape(sessions, state_width // (2 * state_size), 2 * state_size),
        (x_weight, z_weight, bc_weight, dt_weight),
        (dt_bias[None, :], decay_rate[None, :], norm_gain[None, :]),
        out_weight,
        (heads, head_size, state_size),
        shard_count,
        capacity,
    )
    new_store = new_store.reshape(sessions, state_width)
    return (out_sum, new_store)


def solution(mesh):
    return jax.shard_map(
        body,
        mesh=mesh,
        in_specs=(
            P(("groups", "dp"), "mp"),
            P(None, "mp"),
            P(None, "mp"),
            P(None, "mp"),
            P(None, "mp"),
            P("mp"),
            P("mp"),
            P("mp"),
            P("mp", None),
            P(("groups", "dp"), "mp"),
            P("groups"),
            P(("groups", "dp")),
        ),
        out_specs=(P(("groups", "dp", "mp"), None), P(("groups", "dp"), "mp")),
        check_vma=False,
    )
```

```python
import functools

import jax
import jax.numpy as jnp
from jax import lax
from jax.experimental import pallas as pl
from jax.experimental.pallas import tpu as pltpu
from jax.sharding import PartitionSpec as P

F32 = jnp.float32
BF16 = jnp.bfloat16


def rank_within(keys, order):
    earlier = (keys[None, :] == keys[:, None]) & (order[None, :] < order[:, None])
    return jnp.sum(earlier.astype(jnp.int32), axis=1)


def xor_place(me, mask):
    return lax.rem(lax.rem(me, 2) + mask % 2, 2) + 2 * lax.rem(me // 2 + mask // 2, 2)


def layer_kernel(
    heads,
    head_size,
    state_size,
    chunks,
    parts,
    shards,
    scalars,
    tokens_ref,
    store_ref,
    x_ref,
    z_ref,
    bc_ref,
    dtw_ref,
    bias_ref,
    rate_ref,
    gain_ref,
    outw_ref,
    out_ref,
    new_store_ref,
    own,
    sib,
    far,
    diag,
    outbound,
    inbound,
    state_ref,
    outgoing,
    returned,
    acc_ref,
    normed_ref,
    own_sum,
    far_part,
    pair_out,
    pair_in,
    far_out,
    far_in,
    own_sem,
    sib_send,
    sib_recv,
    far_send,
    far_recv,
    diag_send,
    diag_recv,
    store_send,
    store_recv,
    back_send,
    back_recv,
    pair_send,
    pair_recv,
    sum_send,
    sum_recv,
):
    slots = tokens_ref.shape[2]
    depth = tokens_ref.shape[3]
    inner = heads * head_size
    sessions = chunks * parts
    capacity = outbound.shape[1]
    me = lax.axis_index("mp")
    dp = lax.axis_index("dp")
    MESH = pl.DeviceIdType.MESH

    barrier = pltpu.get_barrier_semaphore()
    for mask in range(1, parts):
        pl.semaphore_signal(
            barrier, inc=1, device_id={"mp": xor_place(me, mask)}, device_id_type=MESH
        )
    for k in range(1, shards):
        pl.semaphore_signal(
            barrier, inc=1, device_id={"dp": lax.rem(dp + k, shards)}, device_id_type=MESH
        )
    pl.semaphore_wait(barrier, parts - 1 + shards - 1)

    def remote(src, dst, send, recv, device):
        return pltpu.make_async_remote_copy(
            src_ref=src,
            dst_ref=dst,
            send_sem=send,
            recv_sem=recv,
            device_id=device,
            device_id_type=MESH,
        )

    def far_copy(j):
        return remote(
            tokens_ref.at[:, j], far.at[j], far_send.at[j], far_recv.at[j], {"mp": xor_place(me, 2)}
        )

    def sib_copy(j):
        return remote(
            tokens_ref.at[:, j], sib.at[j], sib_send.at[j], sib_recv.at[j], {"mp": xor_place(me, 1)}
        )

    def diag_copy(j):
        return remote(
            far.at[j], diag.at[j], diag_send.at[j], diag_recv.at[j], {"mp": xor_place(me, 1)}
        )

    def own_copy(j):
        return pltpu.make_async_copy(tokens_ref.at[:, j], own.at[j], own_sem.at[j])

    def store_copy(k):
        return remote(
            outbound.at[k],
            inbound.at[k],
            store_send.at[k],
            store_recv.at[k],
            {"dp": lax.rem(dp + k, shards)},
        )

    def back_copy(k):
        return remote(
            outgoing.at[k],
            returned.at[k],
            back_send.at[k],
            back_recv.at[k],
            {"dp": lax.rem(dp + shards - k, shards)},
        )

    def pair_copy(j):
        return remote(
            pair_out.at[j], pair_in.at[j], pair_send.at[j], pair_recv.at[j], {"mp": xor_place(me, 1)}
        )

    def sum_copy(j):
        return remote(
            far_out.at[j], far_in.at[j], sum_send.at[j], sum_recv.at[j], {"mp": xor_place(me, 2)}
        )

    ahead = min(2, chunks)
    for j in range(ahead):
        far_copy(j).start()
    for j in range(chunks):
        own_copy(j).start()
        sib_copy(j).start()

    def fill_outbound(k):
        for c in range(capacity):
            outbound[k, c] = store_ref[scalars[2 * sessions + k * capacity + c]]

    for k in range(1, shards):
        fill_outbound(k)
        store_copy(k).start()
    for c in range(capacity):
        inbound[0, c] = store_ref[scalars[2 * sessions + c]]

    eye = lax.broadcasted_iota(jnp.int32, (heads, heads), 0) == lax.broadcasted_iota(
        jnp.int32, (heads, heads), 1
    )
    rate_col = jnp.sum(jnp.where(eye, rate_ref[...], 0.0), axis=1, keepdims=True)
    bias_col = jnp.sum(jnp.where(eye, bias_ref[...], 0.0), axis=1, keepdims=True)
    lane = lax.broadcasted_iota(jnp.int32, (slots, slots), 1)
    row = lax.broadcasted_iota(jnp.int32, (slots, slots), 0)
    causal = row >= lane
    low = lane < head_size
    lane8 = lax.broadcasted_iota(jnp.int32, (heads, slots), 1)
    pair = 2 * head_size
    kept_at = 2 * sessions + shards * capacity
    tile = min(512, out_ref.shape[1])
    spread = (row == 2 * (lane % head_size) + lane // head_size).astype(BF16)

    def session(j, step):
        place = lax.rem(lax.rem(me, 2) + lax.rem(step, 2), 2) + 2 * lax.rem(me // 2 + step // 2, 2)
        here = pl.ds(pl.multiple_of(place * slots, slots), slots)
        index = place * chunks + j
        count = scalars[index]
        spot = scalars[sessions + index]
        spot_k = spot // capacity
        spot_c = spot - spot_k * capacity
        bc = acc_ref[here, 2 * inner : 2 * inner + 2 * state_size]
        b_bf = bc[:, :state_size].astype(BF16)
        b_f32 = b_bf.astype(F32)
        c_bf = bc[:, state_size:].astype(BF16)
        slab = acc_ref[here, 2 * inner + 2 * state_size : 2 * inner + 2 * state_size + 128]
        raw = slab.T[:heads, :] + bias_col
        dt_t = jnp.maximum(raw, 0.0) + jnp.log1p(jnp.exp(-jnp.abs(raw)))
        dt_t = jnp.where(lane8 < count, dt_t, 0.0)
        cum_t = dt_t * rate_col
        shift = 1
        while shift < slots:
            moved = pltpu.roll(cum_t, shift, axis=1)
            cum_t = cum_t + jnp.where(lane8 >= shift, moved, 0.0)
            shift *= 2
        last = cum_t[:, slots - 1 : slots]
        weigh_t = jnp.exp(cum_t - last) * dt_t
        fade_t = jnp.exp(-cum_t)
        stacked = jnp.concatenate(
            [cum_t, weigh_t, fade_t, jnp.zeros((slots - 3 * heads, slots), F32)], axis=0
        ).T
        scores = lax.dot_general(
            c_bf, b_bf, (((1,), (1,)), ((), ())), preferred_element_type=F32
        )
        gated_parts = []
        squares = None
        for g in range(heads // 2):
            cols = slice(g * pair, (g + 1) * pair)
            xs = acc_ref[here, cols].astype(BF16)
            zs = acc_ref[here, inner + g * pair : inner + (g + 1) * pair].astype(BF16).astype(F32)
            split = jnp.concatenate(
                [jnp.where(low, xs, jnp.zeros((), BF16)), jnp.where(low, jnp.zeros((), BF16), xs)],
                axis=0,
            )
            mixes = []
            weighed = []
            for h in (2 * g, 2 * g + 1):
                gaps = jnp.where(causal, cum_t[h : h + 1, :] - stacked[:, h : h + 1], -1e30)
                mixes.append((jnp.exp(gaps) * dt_t[h : h + 1, :] * scores).astype(BF16))
                weighed.append((b_f32 * stacked[:, heads + h : heads + h + 1]).astype(BF16))
            y = jnp.dot(jnp.concatenate(mixes, axis=1), split, preferred_element_type=F32)
            rows = slice(g * head_size, (g + 1) * head_size)
            kept = inbound[spot_k, spot_c, rows, :]
            halves = jnp.concatenate([kept[:, :state_size], kept[:, state_size:]], axis=0)
            start = jnp.dot(spread, halves, preferred_element_type=F32).astype(BF16)
            carried = lax.dot_general(
                c_bf, start, (((1,), (1,)), ((), ())), preferred_element_type=F32
            )
            fade0 = stacked[:, 2 * heads + 2 * g : 2 * heads + 2 * g + 1]
            fade1 = stacked[:, 2 * heads + 2 * g + 1 : 2 * heads + 2 * g + 2]
            y = y + carried * jnp.where(low, fade0, fade1)
            grown = lax.dot_general(
                jnp.dot(split, spread, preferred_element_type=F32).astype(BF16),
                jnp.concatenate(weighed, axis=0),
                (((0,), (0,)), ((), ())),
                preferred_element_type=F32,
            )
            keep = jnp.where(
                row[:head_size] < head_size // 2,
                fade_t[2 * g : 2 * g + 1, slots - 1 : slots],
                fade_t[2 * g + 1 : 2 * g + 2, slots - 1 : slots],
            )
            grown = jnp.concatenate([grown[:head_size], grown[head_size:]], axis=1)
            state_ref[index, rows, :] = (keep * kept.astype(F32) + grown).astype(BF16)
            gated = y * (zs * jax.nn.sigmoid(zs))
            part = jnp.sum(gated * gated, axis=1, keepdims=True)
            squares = part if squares is None else squares + part
            gated_parts.append(gated)
        scale = lax.rsqrt(squares * (1.0 / inner) + 1e-05)
        scale = jnp.where(row[:, :1] < count, scale, 0.0)
        for g in range(heads // 2):
            cols = slice(g * pair, (g + 1) * pair)
            normed_ref[pl.ds(pl.multiple_of(step * slots, slots), slots), cols] = (gated_parts[g] * scale * gain_ref[:, cols]).astype(BF16)

    def project(j):
        own_copy(j).wait()
        sib_copy(j).wait_recv()
        diag_copy(j).wait_recv()
        pieces = []
        for step, ref in enumerate((own, sib, far, diag)):
            rows = pl.ds(pl.multiple_of(xor_place(me, step) * depth, depth), depth)
            pieces.append((ref[j].reshape(parts * slots, depth), rows))
        base = 0
        for weight in (x_ref, z_ref, bc_ref, dtw_ref):
            width = weight.shape[1]
            total = None
            for values, rows in pieces:
                piece = jnp.dot(values, weight[rows, :], preferred_element_type=F32)
                total = piece if total is None else total + piece
            if width < 128:
                total = jnp.concatenate(
                    [total, jnp.zeros((total.shape[0], 128 - width), F32)], axis=1
                )
                width = 128
            acc_ref[:, base : base + width] = total
            base += width

    def run_sessions(j):
        @pl.when(j > 0)
        def _():
            combine(j - 1)

        def two_sessions(step, carry):
            session(j, 2 * step)
            session(j, 2 * step + 1)
            return carry

        lax.fori_loop(0, parts // 2, two_sessions, 0)

        @pl.when(j == chunks - 1)
        def _():
            for k in range(1, shards):
                for c in range(capacity):
                    outgoing[k, c] = state_ref[scalars[kept_at + k * capacity + c]]
                back_copy(k).start()

        @pl.loop(0, out_ref.shape[1] // tile)
        def _(t):
            cols = pl.ds(pl.multiple_of(t * tile, tile), tile)
            part = jnp.dot(normed_ref[...], outw_ref[:, cols], preferred_element_type=F32)
            own_sum[j, :, cols] = part[:slots]
            pair_out[j, 0, :, cols] = part[slots : 2 * slots].astype(BF16)
            far_part[:, cols] = part[2 * slots : 3 * slots]
            pair_out[j, 1, :, cols] = part[3 * slots :].astype(BF16)

        pair_copy(j).start()

    def combine(j):
        pair_copy(j).wait_recv()
        far_out[j] = (far_part[...] + pair_in[j, 1].astype(F32)).astype(BF16)
        sum_copy(j).start()

    def round_trip(j, carry):
        @pl.when(j < chunks)
        def _():
            far_copy(j).wait_recv()
            diag_copy(j).start()

        @pl.when(j + ahead < chunks)
        def _():
            far_copy(j + ahead).start()

        @pl.when(j == 1)
        def _():
            for k in range(1, shards):
                store_copy(k).wait_recv()

        @pl.when(j > 0)
        def _():
            run_sessions(j - 1)

        @pl.when(j < chunks)
        def _():
            project(j)

        return carry

    lax.fori_loop(0, chunks + 1, round_trip, 0)

    for c in range(capacity):
        returned[0, c] = state_ref[scalars[kept_at + c]]
    combine(chunks - 1)

    for j in range(chunks):
        sum_copy(j).wait_recv()
        rows = slice(j * slots, (j + 1) * slots)
        out_ref[rows, :] = (
            own_sum[j] + pair_in[j, 0].astype(F32) + far_in[j].astype(F32)
        ).astype(BF16)

    for k in range(1, shards):
        back_copy(k).wait_recv()
    for r in range(sessions):
        spot = scalars[2 * sessions + 2 * shards * capacity + r]
        spot_k = spot // capacity
        new_store_ref[r] = returned[spot_k, spot - spot_k * capacity]

    for j in range(chunks):
        far_copy(j).wait_send()
        sib_copy(j).wait_send()
        diag_copy(j).wait_send()
        pair_copy(j).wait_send()
        sum_copy(j).wait_send()
    for k in range(1, shards):
        store_copy(k).wait_send()
        back_copy(k).wait_send()


def run_layer(scalars, tokens4, store, weights, params, out_weight, sizes, shards, capacity):
    heads, head_size, state_size = sizes
    parts, chunks, slots, depth = tokens4.shape
    inner = heads * head_size
    width = 2 * inner + 2 * state_size + 128
    rows = parts * slots
    model = out_weight.shape[1]
    packed = store.shape[1:]
    vmem = pl.BlockSpec(memory_space=pltpu.VMEM)
    hbm = pl.BlockSpec(memory_space=pl.ANY)
    dma = pltpu.SemaphoreType.DMA
    block = pltpu.VMEM((chunks, parts, slots, depth), BF16)
    exchange = pltpu.VMEM((shards, capacity) + packed, BF16)
    return pl.pallas_call(
        functools.partial(layer_kernel, heads, head_size, state_size, chunks, parts, shards),
        out_shape=(
            jax.ShapeDtypeStruct((chunks * slots, model), BF16),
            jax.ShapeDtypeStruct(store.shape, BF16),
        ),
        in_specs=[pl.BlockSpec(memory_space=pltpu.SMEM), hbm] + [vmem] * 9,
        out_specs=(vmem, vmem),
        scratch_shapes=[
            block,
            block,
            block,
            block,
            exchange,
            exchange,
            pltpu.VMEM((chunks * parts,) + packed, BF16),
            exchange,
            exchange,
            pltpu.VMEM((rows, width), F32),
            pltpu.VMEM((rows, inner), BF16),
            pltpu.VMEM((chunks, slots, model), F32),
            pltpu.VMEM((slots, model), F32),
            pltpu.VMEM((chunks, 2, slots, model), BF16),
            pltpu.VMEM((chunks, 2, slots, model), BF16),
            pltpu.VMEM((chunks, slots, model), BF16),
            pltpu.VMEM((chunks, slots, model), BF16),
        ]
        + [dma((chunks,))] * 7
        + [dma((shards,))] * 4
        + [dma((chunks,))] * 4,
        compiler_params=pltpu.CompilerParams(
            vmem_limit_bytes=62 * 1024 * 1024, collective_id=0, has_side_effects=True
        ),
        cost_estimate=pl.CostEstimate(
            flops=2 * chunks * rows * 4 * depth * width * 4,
            bytes_accessed=64 * 1024 * 1024,
            transcendentals=chunks * rows * heads * slots,
        ),
        name="layer",
    )(scalars, tokens4, store, *weights, *params, out_weight)


def body(
    tokens,
    x_weight,
    z_weight,
    bc_weight,
    dt_weight,
    dt_bias,
    decay_rate,
    norm_gain,
    out_weight,
    store_states,
    home_rows,
    event_counts,
):
    shard_count = lax.axis_size("dp")
    parts = lax.axis_size("mp")
    me = lax.axis_index("dp")
    sessions = store_states.shape[0]
    state_width = store_states.shape[1]
    capacity = max(2, (sessions + shard_count - 1) // shard_count)
    slot_count = shard_count * capacity
    heads = dt_bias.shape[0]
    inner = x_weight.shape[1]
    head_size = inner // heads
    state_size = bc_weight.shape[1] // 2
    depth = tokens.shape[1]
    slots = tokens.shape[0] // sessions
    chunks = sessions // parts

    tokens4 = tokens.reshape(parts, chunks, slots, depth)

    positions = jnp.arange(sessions, dtype=jnp.int32)
    store_rows = me * sessions + positions
    everyone = jnp.arange(home_rows.shape[0], dtype=jnp.int32)
    owner = jnp.sum(
        (home_rows[None, :] == store_rows[:, None]).astype(jnp.int32) * everyone[None, :], axis=1
    )
    server = owner // sessions
    to_server = (server - me + shard_count) % shard_count
    row_slot = to_server * capacity + rank_within(server, positions)
    wanted = lax.dynamic_slice_in_dim(home_rows, me * sessions, sessions)
    home_shard = wanted // sessions
    from_home = (me - home_shard + shard_count) % shard_count
    session_slot = from_home * capacity + rank_within(home_shard, wanted % sessions)

    all_slots = jnp.arange(slot_count, dtype=jnp.int32)

    def holder(slot_of):
        chosen = slot_of[None, :] == all_slots[:, None]
        return jnp.sum(chosen.astype(jnp.int32) * positions[None, :], axis=1)

    scalars = jnp.concatenate(
        [event_counts, session_slot, holder(row_slot), holder(session_slot), row_slot]
    )
    out_sum, new_store = run_layer(
        scalars,
        tokens4,
        store_states.reshape(sessions, state_width // (2 * state_size), 2 * state_size),
        (x_weight, z_weight, bc_weight, dt_weight),
        (dt_bias[None, :], decay_rate[None, :], norm_gain[None, :]),
        out_weight,
        (heads, head_size, state_size),
        shard_count,
        capacity,
    )
    new_store = new_store.reshape(sessions, state_width)
    return (out_sum, new_store)


def solution(mesh):
    return jax.shard_map(
        body,
        mesh=mesh,
        in_specs=(
            P(("groups", "dp"), "mp"),
            P(None, "mp"),
            P(None, "mp"),
            P(None, "mp"),
            P(None, "mp"),
            P("mp"),
            P("mp"),
            P("mp"),
            P("mp", None),
            P(("groups", "dp"), "mp"),
            P("groups"),
            P(("groups", "dp")),
        ),
        out_specs=(P(("groups", "dp", "mp"), None), P(("groups", "dp"), "mp")),
        check_vma=False,
    )
```
